256 devices in a mesh: pair: 8 (over x, core), grow: 4 (over y), gcol: 8 (over z).
Axes of the slice: x: 4, y: 4, z: 8, core: 2. Of those that a mesh axis runs over, the one named last changes fastest.
Arguments:
- core_matrix: bfloat16 [12288, 12288], P('grow', 'gcol'), may hold values from -0.00048828125 to 0.00048828125
- pair_panels: bfloat16 [48, 32, 12288], P('pair', None, ('grow', 'gcol')), may hold values from -6 to 6
- amplitudes: bfloat16 [48, 32, 32], P('pair'), may hold values from -0.1875 to 0.1875
- pair_widths: int32 [48], P('pair'), may hold values from 8 to 32
- batch_plan: int32 [48], P('pair'), may hold values from 0 to 47, each once
Outputs:
- residual: float32 [48, 1024], P('pair', ('grow', 'gcol'))
The draws below stay inside these ranges and needn't reach their ends.
Inputs may be any that keep to these rules, and one draw needn't show every extreme that they name: batch_plan names every pair exactly once.
All inputs are finite; a program needn't handle non-finite values.
Results may differ from the reference program's by a relative error of at most 0.015.
Values may be sent and summed in bfloat16 or wider, within the bound.
No kernel may reach another device: no remote copies, remote signals or barrier semaphores. Data moves between devices by JAX's collectives and lax.ppermute only.
A program may use at most 64 MiB of HBM per device.

```python
import jax
import jax.numpy as jnp
from jax import lax

NG = 12288
NPNO = 32
PAIRS = 48


def set_ends(drawn, key, low, top_value):
    longest = drawn.shape.index(max(drawn.shape))
    spots = []
    for shift in (0, 1):
        where = [jax.random.randint(jax.random.fold_in(key, axis), (), 0, length) for axis, length in enumerate(drawn.shape)]
        where[longest] = (where[longest] + shift) % drawn.shape[longest]
        spots.append(tuple(where))
    return drawn.at[spots[0]].set(low).at[spots[1]].set(top_value)


def shard_levels(rng, dims, split, smallest, high):
    factor_of = 1.0
    for axis_at, shards_of in split:
        draws = jax.random.uniform(jax.random.fold_in(jax.random.fold_in(rng, 6), axis_at), (shards_of,), jnp.float32, smallest / len(split), high / len(split))
        factor_of = factor_of * jnp.repeat(jnp.exp(draws), dims[axis_at] // shards_of).reshape((-1,) + (1,) * (len(dims) - 1 - axis_at))
    return factor_of


def gaussian(own_key, shape, scale, reach, shards=(), kind=jnp.bfloat16):
    drawn = scale * jax.random.normal(own_key, shape, jnp.float32)
    if shards:
        drawn = drawn * shard_levels(own_key, shape, shards, -0.22, 0.18)
    return jnp.clip(drawn, -reach, reach).astype(kind)


def setup_inputs(seed: int = 0) -> dict:
    splits = jax.random.split(jax.random.key(seed), 6)
    return {
        "core_matrix": gaussian(splits[0], (NG, NG), (NG * NG) ** -0.5, 0.00048828125, ((0, 4), (1, 8))),
        "pair_panels": gaussian(splits[1], (PAIRS, NPNO, NG), 1.0, 6.0, ((0, 8), (2, 32))),
        "amplitudes": gaussian(splits[2], (PAIRS, NPNO, NPNO), (NPNO * NPNO) ** -0.5, 0.1875, ((0, 8),)),
        "pair_widths": set_ends(jax.random.randint(splits[3], (PAIRS,), NPNO // 4, NPNO + 1), jax.random.fold_in(splits[3], 1), NPNO // 4, NPNO).astype(jnp.int32),
        "batch_plan": jax.random.permutation(splits[4], PAIRS).astype(jnp.int32),
    }


def pair_term(core_matrix, panel, amps, width):
    live = (lax.iota(jnp.int32, NPNO) < width).astype(jnp.bfloat16)
    masked = amps * live[:, None] * live[None, :]
    projected = jnp.dot(masked, panel, preferred_element_type=jnp.float32).astype(jnp.bfloat16)
    block = min(512, NG)
    count = NG // block

    def step(total, which):
        start = (which * block).astype(jnp.int32)
        left = lax.dynamic_slice_in_dim(panel, start, block, 1)
        core_rows = lax.dynamic_slice_in_dim(core_matrix, start, block, 0)
        coupled = lax.dot_general(left, projected, (((0,), (0,)), ((), ())), preferred_element_type=jnp.float32).astype(jnp.bfloat16)
        coupled = lax.optimization_barrier(coupled)
        weighted = (core_rows.astype(jnp.float32) * coupled.astype(jnp.float32)).astype(jnp.bfloat16)
        back = lax.dot_general(weighted, panel, (((1,), (1,)), ((), ())), preferred_element_type=jnp.float32).astype(jnp.bfloat16)
        total = total + jnp.dot(left, back, preferred_element_type=jnp.float32)
        return total, None

    total, _ = lax.scan(step, jnp.zeros((NPNO, NPNO), jnp.float32), jnp.arange(count, dtype=jnp.int32))
    keep = live.astype(jnp.float32)
    return (total * keep[:, None] * keep[None, :]).reshape(NPNO * NPNO)


def reference(core_matrix, pair_panels, amplitudes, pair_widths, batch_plan):
    def single(pair_id):
        return pair_term(core_matrix, pair_panels[pair_id], amplitudes[pair_id], pair_widths[pair_id])

    return lax.map(single, batch_plan)
```

```python
import jax
import jax.numpy as jnp
from jax import lax
from jax.experimental import pallas as pl
from jax.experimental.pallas import tpu as pltpu
from jax.sharding import PartitionSpec as P

F32 = jnp.float32
BF16 = jnp.bfloat16
NN = (((1,), (0,)), ((), ()))
NT = (((1,), (1,)), ((), ()))
TN = (((0,), (0,)), ((), ()))


def dot(a, b, dims):
    return lax.dot_general(a, b, dims, preferred_element_type=F32)


def shift(size, by):
    return [(i, (i + by) % size) for i in range(size)]


def ring_chunks(own, axis):
    size = lax.axis_size(axis)
    chunks, back = [own], [0]
    right = left = own
    for step in range(1, size // 2 + 1):
        right = lax.ppermute(right, axis, shift(size, 1))
        chunks.append(right)
        back.append(step)
        if step < size - step:
            left = lax.ppermute(left, axis, shift(size, -1))
            chunks.append(left)
            back.append(-step)
    return chunks, back


def column_chunks(own, rows, cols):
    per = rows
    pairs = [(per * j + g, g * cols + j) for g in range(rows) for j in range(cols)]
    first = lax.ppermute(own, ("grow", "gcol"), pairs)
    return [first] + [lax.ppermute(first, "grow", shift(rows, d)) for d in range(1, rows)]


def pair_kernel(place, core_ref, left_ref, r0, r1, r2, r3, amps_ref, live_ref, out_ref, right_ref, proj_ref):
    step, pair = pl.program_id(0), pl.program_id(1)
    chunk = left_ref.shape[-1]

    @pl.when((step == 0) & (pair == 0))
    def _():
        for d, ref in enumerate((r0, r1, r2, r3)):
            at = pl.multiple_of(lax.rem(place[0] + 4 - d, 4) * chunk, 128)
            right_ref[:, :, pl.ds(at, chunk)] = ref[...]

    @pl.when(step == 0)
    def _():
        proj_ref[pair] = dot(amps_ref[pair], right_ref[pair], NN).astype(BF16)
        out_ref[pair] = jnp.zeros(out_ref.shape[1:], F32)

    left = left_ref[0, 0]
    coupled = dot(left, proj_ref[pair], TN).astype(BF16)
    weighted = core_ref[...] * coupled
    back = dot(right_ref[pair], weighted, NT).astype(BF16)
    out_ref[pair] += dot(left, back, NT)

    @pl.when(step == pl.num_programs(0) - 1)
    def _():
        out_ref[pair] = out_ref[pair] * live_ref[pair]


def local(core_matrix, pair_panels, amplitudes, pair_widths, batch_plan):
    pairs, depth, chunk = pair_panels.shape
    rows, cols = lax.axis_size("grow"), lax.axis_size("gcol")
    live = lax.broadcasted_iota(jnp.int32, (pairs, depth), 1) < pair_widths[:, None]
    live = live[:, :, None] & live[:, None, :]
    masked = jnp.where(live, amplitudes, 0)
    right = column_chunks(pair_panels, rows, cols)
    chunks, back = ring_chunks(pair_panels, "gcol")
    left = jnp.stack(chunks)
    origin = lax.rem(lax.axis_index("gcol") + cols - jnp.array(back, jnp.int32), cols)
    place = jnp.concatenate([lax.axis_index("grow")[None], origin])
    whole = pl.BlockSpec(memory_space=pltpu.VMEM)
    terms = pl.pallas_call(
        pair_kernel,
        out_shape=jax.ShapeDtypeStruct((pairs, depth, depth), F32),
        grid_spec=pltpu.PrefetchScalarGridSpec(
            num_scalar_prefetch=1,
            grid=(cols, pairs),
            in_specs=[
                pl.BlockSpec((chunk, core_matrix.shape[1]), lambda s, p, at: (at[1 + s], 0)),
                pl.BlockSpec((1, 1, depth, chunk), lambda s, p, at: (s, p, 0, 0)),
            ]
            + [whole] * 6,
            out_specs=whole,
            scratch_shapes=[
                pltpu.VMEM((pairs, depth, rows * chunk), BF16),
                pltpu.VMEM((pairs, depth, rows * chunk), BF16),
            ],
        ),
        compiler_params=pltpu.CompilerParams(vmem_limit_bytes=48 << 20),
    )(place, core_matrix, left, *right, masked, live.astype(F32))
    parts = terms.reshape(pairs, rows * cols, depth * depth // (rows * cols))
    parts = parts.transpose(1, 0, 2).reshape(rows * cols, -1)
    mine = lax.all_to_all(parts, ("grow", "gcol"), 0, 0, tiled=True).sum(axis=0)
    copies = jnp.broadcast_to(mine, (lax.axis_size("pair"), *mine.shape))
    every = lax.all_to_all(copies, "pair", 0, 0, tiled=True)
    return jnp.take(every.reshape(-1, depth * depth // (rows * cols)), batch_plan, axis=0)


def solution(mesh):
    in_specs = (
        P("grow", "gcol"),
        P("pair", None, ("grow", "gcol")),
        P("pair", None, None),
        P("pair"),
        P("pair"),
    )
    out_specs = P("pair", ("grow", "gcol"))
    return jax.shard_map(local, mesh=mesh, in_specs=in_specs, out_specs=out_specs, check_vma=False)
```

```python
import functools

import jax
import jax.numpy as jnp
from jax import lax
from jax.experimental import pallas as pl
from jax.experimental.pallas import tpu as pltpu
from jax.sharding import PartitionSpec as P

F32 = jnp.float32
BF16 = jnp.bfloat16
NN = (((1,), (0,)), ((), ()))
NT = (((1,), (1,)), ((), ()))
BLOCK = 8
TILE = 64
SPAN = 512
LIMIT = 14


def dot(a, b, dims):
    return lax.dot_general(a, b, dims, preferred_element_type=F32)


def shift(size, by):
    return [(i, (i + by) % size) for i in range(size)]


def column_chunks(own, rows, cols):
    pairs = [(rows * j + g, g * cols + j) for g in range(rows) for j in range(cols)]
    first = lax.ppermute(own, ("grow", "gcol"), pairs)
    return [first] + [lax.ppermute(first, "grow", shift(rows, d)) for d in range(1, rows)]


def block_table(widths, depth):
    pairs = widths.shape[0]
    group = widths // BLOCK
    count = BLOCK * group * (group + 1) // 2 + (widths - BLOCK * group) * (group + 1)
    earlier = jnp.arange(pairs)[:, None] > jnp.arange(pairs)[None, :]
    start = jnp.sum(jnp.where(earlier, count[None, :], 0), axis=1)
    at = lax.iota(jnp.int32, 512)
    pair = jnp.sum((at[:, None] >= start[None, 1:]).astype(jnp.int32), axis=1)
    inside = at - jnp.sum(jnp.where(pair[:, None] == jnp.arange(pairs)[None, :], start[None, :], 0), axis=1)
    level = (inside >= 8).astype(jnp.int32) + (inside >= 24) + (inside >= 48)
    rest = inside - 4 * level * (level + 1)
    step = rest // (level + 1)
    first = pair * depth + BLOCK * (rest - step * (level + 1))
    partner = pair * depth + BLOCK * level + step
    total = jnp.sum(count)
    return jnp.where(at < total, 256 * first + partner, 0), total


def stage_kernel(backs, opens, closes, place, table, core_ref, *refs):
    refs = list(refs)
    n_chunks = len(backs)
    chunk_refs = [refs.pop(0) for _ in backs]
    if closes:
        right_chunks = [refs.pop(0) for _ in range(4)]
        amps_ref, live_ref = refs.pop(0), refs.pop(0)
    if not opens:
        refs.pop(0)
    m_ref = refs.pop(0)
    if closes:
        out_ref = refs.pop(0)
    core_v, panel, rho, sems = refs[:4]
    pairs, depth, chunk = chunk_refs[0].shape
    copies = []
    for u in range(n_chunks):
        rows = pl.ds(pl.multiple_of(lax.rem(place[2] + 8 - backs[u], 8) * chunk, chunk), chunk)
        copies.append(pltpu.make_async_copy(core_ref.at[rows], core_v.at[pl.ds(u * chunk, chunk)], sems.at[u]))
        copies[-1].start()
    for u in range(n_chunks):
        for p in range(pairs):
            panel[p * depth : (p + 1) * depth, u * chunk : (u + 1) * chunk] = chunk_refs[u][p].astype(F32)
    for copy in copies:
        copy.wait()
    total = place[0]

    def density(code):
        first = pl.multiple_of(lax.shift_right_logical(code, 8), BLOCK)
        return panel[pl.ds(first, BLOCK), :] * panel[pl.ds(lax.bitwise_and(code, 255), 1), :]

    def tile(start, blocks):
        def two(i, carry):
            both = [density(table[start + 2 * i]), density(table[start + 2 * i + 1])]
            rho[pl.ds(pl.multiple_of(16 * i, 16), 16), :] = jnp.concatenate(both, axis=0).astype(BF16)
            return carry

        lax.fori_loop(0, blocks // 2, two, 0, unroll=8)
        at = pl.ds(pl.multiple_of(start * BLOCK, 256), blocks * BLOCK)
        for s in range(0, core_v.shape[1], SPAN):
            term = dot(rho[: blocks * BLOCK, :], core_v[:, s : s + SPAN], NN)
            if opens:
                m_ref[at, s : s + SPAN] = term
            else:
                m_ref[at, s : s + SPAN] += term

    tiles = (total + TILE // 2 - 1) // TILE

    def full(t, carry):
        tile(t * TILE, TILE)
        return carry

    lax.fori_loop(0, tiles, full, 0)

    @pl.when(total > tiles * TILE)
    def _():
        tile(tiles * TILE, TILE // 2)

    if closes:
        right, proj, acc = refs[4:]
        for d, ref in enumerate(right_chunks):
            at = pl.multiple_of(lax.rem(place[1] + 4 - d, 4) * chunk, 128)
            right[:, :, pl.ds(at, chunk)] = ref[...]
        for p in range(pairs):
            rows = slice(p * depth, (p + 1) * depth)
            proj[rows, :] = dot(amps_ref[p], right[p], NN).astype(BF16).astype(F32)
        acc[...] = jnp.zeros_like(acc)

        def spread(i, carry):
            code = table[i]
            first = pl.multiple_of(lax.shift_right_logical(code, 8), BLOCK)
            partner = lax.bitwise_and(code, 255)
            term = m_ref[pl.ds(pl.multiple_of(i * BLOCK, BLOCK), BLOCK), :]
            acc[pl.ds(first, BLOCK), :] += term * proj[pl.ds(partner, 1), :]

            @pl.when(partner >= first + BLOCK)
            def _():
                mirrored = jnp.sum(term * proj[pl.ds(first, BLOCK), :], axis=0, keepdims=True)
                acc[pl.ds(partner, 1), :] += mirrored

            return carry

        lax.fori_loop(0, total, spread, 0)
        for p in range(pairs):
            rows = slice(p * depth, (p + 1) * depth)
            out_ref[p] = dot(acc[rows, :].astype(BF16), right[p], NT) * live_ref[p]


def stage(place, table, core, chunks, backs, state, ending=None):
    pairs, depth, chunk = chunks[0].shape
    width = core.shape[1]
    opens, closes = state is None, ending is not None
    inner = chunk * len(chunks)
    vmem = pl.BlockSpec(memory_space=pltpu.VMEM)
    smem = pl.BlockSpec(memory_space=pltpu.SMEM)
    args = [place, table, core, *chunks]
    specs = [smem, smem, pl.BlockSpec(memory_space=pltpu.HBM)] + [vmem] * len(chunks)
    if closes:
        args += ending
        specs += [vmem] * len(ending)
    if not opens:
        args.append(state)
        specs.append(vmem)
    rows = pairs * 80 * BLOCK
    scratch = [
        pltpu.VMEM((inner, width), BF16),
        pltpu.VMEM((pairs * depth, inner), F32),
        pltpu.VMEM((TILE * BLOCK, inner), BF16),
        pltpu.SemaphoreType.DMA((len(chunks),)),
    ]
    if closes:
        scratch += [
            pltpu.VMEM((pairs, depth, width), BF16),
            pltpu.VMEM((pairs * depth, width), F32),
            pltpu.VMEM((pairs * depth, width), F32),
        ]
    out = [pltpu.VMEM((rows, width), F32)]
    if closes:
        out.append(jax.ShapeDtypeStruct((pairs, depth, depth), F32))
    return pl.pallas_call(
        functools.partial(stage_kernel, backs, opens, closes),
        out_shape=out,
        in_specs=specs,
        out_specs=[vmem] * len(out),
        scratch_shapes=scratch,
        input_output_aliases={} if opens else {len(args) - 1: 0},
        cost_estimate=pl.CostEstimate(flops=2 * 2048 * inner * width, bytes_accessed=2 * inner * width, transcendentals=0),
        compiler_params=pltpu.CompilerParams(vmem_limit_bytes=LIMIT << 20),
    )(*args)[-1]


def local(core_matrix, pair_panels, amplitudes, pair_widths, batch_plan):
    pairs, depth, chunk = pair_panels.shape
    rows, cols = lax.axis_size("grow"), lax.axis_size("gcol")
    live = lax.broadcasted_iota(jnp.int32, (pairs, depth), 1) < pair_widths[:, None]
    live = live[:, :, None] & live[:, None, :]
    masked = jnp.where(live, amplitudes, 0)
    table, total = block_table(pair_widths, depth)
    place = jnp.stack([total, lax.axis_index("grow"), lax.axis_index("gcol")])
    masked, live, table, place = lax.optimization_barrier((masked, live.astype(F32), table, place))
    core_matrix = pltpu.with_memory_space_constraint(core_matrix, pltpu.HBM)
    run = functools.partial(stage, place, table, core_matrix)

    right = left = pair_panels
    state = run([pair_panels], (0,), None)
    for step in (1, 2):
        right = lax.ppermute(right, "gcol", shift(cols, 1))
        left = lax.ppermute(left, "gcol", shift(cols, -1))
        state = run([right, left], (step, -step), state)
    right = lax.ppermute(right, "gcol", shift(cols, 1))
    left = lax.ppermute(left, "gcol", shift(cols, -1))
    last = lax.ppermute(right, "gcol", shift(cols, 1))
    ending = [*column_chunks(pair_panels, rows, cols), masked, live]
    terms = run([right, left, last], (3, -3, 4), state, ending)
    parts = terms.reshape(pairs, rows * cols, depth * depth // (rows * cols))
    parts = parts.transpose(1, 0, 2).reshape(rows * cols, -1)
    mine = lax.all_to_all(parts, ("grow", "gcol"), 0, 0, tiled=True).sum(axis=0)
    copies = jnp.broadcast_to(mine, (lax.axis_size("pair"), *mine.shape))
    every = lax.all_to_all(copies, "pair", 0, 0, tiled=True)
    every = every.reshape(-1, depth * depth // (rows * cols))
    return every.at[batch_plan].get(mode="promise_in_bounds")


def solution(mesh):
    in_specs = (
        P("grow", "gcol"),
        P("pair", None, ("grow", "gcol")),
        P("pair", None, None),
        P("pair"),
        P("pair"),
    )
    out_specs = P("pair", ("grow", "gcol"))
    return jax.shard_map(local, mesh=mesh, in_specs=in_specs, out_specs=out_specs, check_vma=False)
```

```python
import functools

import jax
import jax.numpy as jnp
from jax import lax
from jax.experimental import pallas as pl
from jax.experimental.pallas import tpu as pltpu
from jax.sharding import PartitionSpec as P

F32 = jnp.float32
BF16 = jnp.bfloat16
NN = (((1,), (0,)), ((), ()))
NT = (((1,), (1,)), ((), ()))
BLOCK = 8
TILE = 64
LIMIT = 24


def dot(a, b, dims):
    return lax.dot_general(a, b, dims, preferred_element_type=F32)


def shift(size, by):
    return [(i, (i + by) % size) for i in range(size)]


def column_chunks(own, rows, cols):
    pairs = [(rows * j + g, g * cols + j) for g in range(rows) for j in range(cols)]
    first = lax.ppermute(own, ("grow", "gcol"), pairs)
    return [first] + [lax.ppermute(first, "grow", shift(rows, d)) for d in range(1, rows)]


def fill_table(widths, table, depth):
    at = jnp.int32(0)
    for p in range(widths.shape[0]):

        def partner(c, at):
            level = lax.shift_right_logical(c, 3)
            for i in range(depth // BLOCK):
                table[at + i] = 256 * (p * depth + BLOCK * i) + p * depth + c
            return at + level + 1

        at = lax.fori_loop(0, widths[p], partner, at)

    def clear(i, carry):
        table[at + i] = 0
        return carry

    lax.fori_loop(0, 2 * TILE, clear, 0, unroll=8)
    table[table.shape[0] - 1] = at


def row_targets(widths, total, start, rows, depth):
    at = start * BLOCK + lax.broadcasted_iota(jnp.int32, (1, rows), 1)
    block, offset = lax.shift_right_logical(at, 3), lax.bitwise_and(at, BLOCK - 1)
    begin = jnp.int32(0)
    base, inside = jnp.zeros_like(at), block
    for p in range(widths.shape[0] - 1):
        group = lax.shift_right_logical(widths[p], 3)
        begin = begin + 4 * group * (group + 1) + (widths[p] - BLOCK * group) * (group + 1)
        base = jnp.where(block >= begin, (p + 1) * depth, base)
        inside = jnp.where(block >= begin, block - begin, inside)
    level = jnp.where(inside >= 8, 1, 0) + jnp.where(inside >= 24, 1, 0) + jnp.where(inside >= 48, 1, 0)
    rest = inside - 4 * level * (level + 1)
    scale = jnp.where(level == 0, 256, jnp.where(level == 1, 128, jnp.where(level == 2, 86, 64)))
    step = lax.shift_right_logical(rest * scale, 8)
    first = BLOCK * (rest - step * (level + 1))
    here = block < total
    return (
        jnp.where(here, base + first + offset, -1),
        jnp.where(here & (first < BLOCK * level), base + BLOCK * level + step, -1),
    )


def stage_kernel(backs, opens, closes, *refs):
    refs = list(refs)
    widths, core_ref = refs.pop(0), refs.pop(0)
    chunk_refs = [refs.pop(0) for _ in backs]
    if closes:
        right_chunks = [refs.pop(0) for _ in range(4)]
        amps_ref = refs.pop(0)
    if not opens:
        table = refs.pop(0)
        refs.pop(0)
    m_ref = refs.pop(0)
    if opens:
        table = refs.pop(0)
    if closes:
        out_ref = refs.pop(0)
    core_v, panel, rho_a, rho_b, sems = refs[:5]
    pairs, depth, chunk = chunk_refs[0].shape
    me = lax.axis_index("gcol")
    copies = []
    if opens:
        own = refs[5]
        copies.append(pltpu.make_async_copy(chunk_refs[0], own, sems.at[len(backs)]))
        copies[-1].start()
        chunk_refs = [own]
    for u, back in enumerate(backs):
        rows = pl.ds(pl.multiple_of(lax.rem(me + 8 - back, 8) * chunk, chunk), chunk)
        copies.append(pltpu.make_async_copy(core_ref.at[rows], core_v.at[pl.ds(u * chunk, chunk)], sems.at[u]))
        copies[-1].start()
    if opens:
        fill_table(widths, table, depth)
        copies.pop(0).wait()
    for u in range(len(backs)):
        for p in range(pairs):
            panel[p * depth : (p + 1) * depth, u * chunk : (u + 1) * chunk] = chunk_refs[u][p].astype(F32)
    total = table[table.shape[0] - 1]

    def density(code):
        first = pl.multiple_of(lax.shift_right_logical(code, 8), BLOCK)
        return panel[pl.ds(first, BLOCK), :] * panel[pl.ds(lax.bitwise_and(code, 255), 1), :]

    def build(rho, start):
        for i in range(TILE // 2):
            both = [density(table[start + 2 * i]), density(table[start + 2 * i + 1])]
            rho[16 * i : 16 * (i + 1), :] = jnp.concatenate(both, axis=0).astype(BF16)

    if closes:
        right, proj, term_a, term_b, acc = refs[5:]
        for d, ref in enumerate(right_chunks):
            at = pl.multiple_of(lax.rem(lax.axis_index("grow") + 4 - d, 4) * chunk, 128)
            for p in range(pairs):
                right[p * depth : (p + 1) * depth, pl.ds(at, chunk)] = ref[p]
        live = []
        for p in range(pairs):
            rows = slice(p * depth, (p + 1) * depth)
            spot = [lax.broadcasted_iota(jnp.int32, (depth, depth), k) < widths[p] for k in (0, 1)]
            live.append(spot[0] & spot[1])
            masked = jnp.where(live[p], amps_ref[p].astype(F32), 0.0).astype(BF16)
            proj[rows, :] = dot(masked, right[rows, :], NN).astype(BF16).astype(F32)
        acc[...] = jnp.zeros_like(acc)

    def finish(start, blocks):
        def two(i, carry):
            plain, mirrored = [], []
            for k in range(2):
                code = table[start + 2 * i + k]
                first = pl.multiple_of(lax.shift_right_logical(code, 8), BLOCK)
                at = pl.multiple_of((start + 2 * i + k) * BLOCK, BLOCK)
                term = m_ref[pl.ds(at, BLOCK), :]
                plain.append(term * proj[pl.ds(lax.bitwise_and(code, 255), 1), :])
                mirrored.append(term * proj[pl.ds(first, BLOCK), :])
            at = pl.ds(pl.multiple_of(16 * i, 16), 16)
            term_a[at, :] = jnp.concatenate(plain, axis=0).astype(BF16)
            term_b[at, :] = jnp.concatenate(mirrored, axis=0).astype(BF16)
            return carry

        lax.fori_loop(0, blocks // 2, two, 0, unroll=4)
        rows = blocks * BLOCK
        orbital = lax.broadcasted_iota(jnp.int32, (pairs * depth, rows), 0)
        for target, term in zip(row_targets(widths, total, start, rows, depth), (term_a, term_b)):
            pick = jnp.where(orbital == target, 1.0, 0.0).astype(BF16)
            acc[...] += dot(pick, dot(term[:rows, :], right[...], NT).astype(BF16), NN)

    def multiply(rho, start, blocks):
        at = pl.ds(pl.multiple_of(start * BLOCK, 256), blocks * BLOCK)
        term = dot(rho[: blocks * BLOCK, :], core_v[...], NN)
        if opens:
            m_ref[at, :] = term
        else:
            m_ref[at, :] += term
        if closes:
            finish(start, blocks)

    def step(rho, later, t):
        build(later, (t + 1) * TILE)
        multiply(rho, t * TILE, TILE)

    build(rho_a, 0)
    for copy in copies:
        copy.wait()
    tiles = (total + TILE // 2 - 1) // TILE

    def two_steps(i, carry):
        step(rho_a, rho_b, 2 * i)

        @pl.when(2 * i + 1 < tiles)
        def _():
            step(rho_b, rho_a, 2 * i + 1)

        return carry

    lax.fori_loop(0, (tiles + 1) // 2, two_steps, 0)
    odd = lax.rem(tiles, 2)
    for k, rho in enumerate((rho_a, rho_b)):

        @pl.when((total > tiles * TILE) & (odd == k))
        def _(rho=rho):
            multiply(rho, tiles * TILE, TILE // 2)

    if closes:
        for p in range(pairs):
            rows = slice(p * depth, (p + 1) * depth)
            out_ref[:, rows] = jnp.where(live[p], acc[rows, rows], 0.0)


def stage(widths, core, chunks, backs, state, ending=()):
    pairs, depth, chunk = chunks[0].shape
    width = core.shape[1]
    opens, closes = state is None, len(ending) > 0
    inner = chunk * len(chunks)
    vmem = pl.BlockSpec(memory_space=pltpu.VMEM)
    smem = pl.BlockSpec(memory_space=pltpu.SMEM)
    hbm = pl.BlockSpec(memory_space=pltpu.HBM)
    args = [widths, core, *chunks, *ending]
    specs = [smem, hbm] + [hbm if opens else vmem] * len(chunks) + [vmem] * len(ending)
    if not opens:
        args += [state[1], state[0]]
        specs += [smem, vmem]
    rows = pairs * depth
    most = pairs * BLOCK * sum(range(1, depth // BLOCK + 1))
    scratch = [
        pltpu.VMEM((inner, width), BF16),
        pltpu.VMEM((rows, inner), F32),
        pltpu.VMEM((TILE * BLOCK, inner), BF16),
        pltpu.VMEM((TILE * BLOCK, inner), BF16),
        pltpu.SemaphoreType.DMA((len(chunks) + 1,)),
    ]
    out, out_specs = [pltpu.VMEM((most * BLOCK, width), F32)], [vmem]
    if opens:
        scratch.append(pltpu.VMEM((pairs, depth, chunk), BF16))
        out.append(jax.ShapeDtypeStruct((most + 3 * TILE,), jnp.int32))
        out_specs.append(smem)
    if closes:
        scratch += [
            pltpu.VMEM((rows, width), BF16),
            pltpu.VMEM((rows, width), F32),
            pltpu.VMEM((TILE * BLOCK, width), BF16),
            pltpu.VMEM((TILE * BLOCK, width), BF16),
            pltpu.VMEM((rows, rows), F32),
        ]
        out.append(jax.ShapeDtypeStruct((depth, rows), F32))
        out_specs.append(vmem)
    results = pl.pallas_call(
        functools.partial(stage_kernel, backs, opens, closes),
        out_shape=out,
        in_specs=specs,
        out_specs=out_specs,
        scratch_shapes=scratch,
        input_output_aliases={} if opens else {len(args) - 1: 0},
        cost_estimate=pl.CostEstimate(flops=2 * 2048 * inner * width, bytes_accessed=2 * inner * width, transcendentals=0),
        compiler_params=pltpu.CompilerParams(vmem_limit_bytes=LIMIT << 20),
    )(*args)
    if closes:
        return results[1]
    return (results[0], results[1] if opens else state[1])


def local(core_matrix, pair_panels, amplitudes, pair_widths, batch_plan):
    rows, cols = lax.axis_size("grow"), lax.axis_size("gcol")
    core_matrix = pltpu.with_memory_space_constraint(core_matrix, pltpu.HBM)
    run = functools.partial(stage, pair_widths, core_matrix)

    right = left = pair_panels
    state = run([pltpu.with_memory_space_constraint(pair_panels, pltpu.HBM)], (0,), None)
    for step in (1, 2):
        right = lax.ppermute(right, "gcol", shift(cols, 1))
        left = lax.ppermute(left, "gcol", shift(cols, -1))
        state = run([right, left], (step, -step), state)
    right = lax.ppermute(right, "gcol", shift(cols, 1))
    left = lax.ppermute(left, "gcol", shift(cols, -1))
    last = lax.ppermute(right, "gcol", shift(cols, 1))
    ending = [*column_chunks(pair_panels, rows, cols), amplitudes]
    parts = run([right, left, last], (3, -3, 4), state, ending)
    mine = lax.all_to_all(parts, ("grow", "gcol"), 0, 0, tiled=True).sum(axis=0)
    copies = jnp.broadcast_to(mine, (lax.axis_size("pair"), *mine.shape))
    every = lax.all_to_all(copies, "pair", 0, 0, tiled=True)
    every = every.reshape(-1, parts.shape[0])
    return every.at[batch_plan].get(mode="promise_in_bounds")


def solution(mesh):
    in_specs = (
        P("grow", "gcol"),
        P("pair", None, ("grow", "gcol")),
        P("pair", None, None),
        P("pair"),
        P("pair"),
    )
    out_specs = P("pair", ("grow", "gcol"))
    return jax.shard_map(local, mesh=mesh, in_specs=in_specs, out_specs=out_specs, check_vma=False)
```

```python
import functools

import jax
import jax.numpy as jnp
from jax import lax
from jax.experimental import pallas as pl
from jax.experimental.pallas import tpu as pltpu
from jax.sharding import PartitionSpec as P

F32 = jnp.float32
BF16 = jnp.bfloat16
NN = (((1,), (0,)), ((), ()))
NT = (((1,), (1,)), ((), ()))
TN = (((0,), (0,)), ((), ()))
BLOCK = 8
TILE = 64
LIMIT = 24


def dot(a, b, dims):
    return lax.dot_general(a, b, dims, preferred_element_type=F32)


def shift(size, by):
    return [(i, (i + by) % size) for i in range(size)]


def column_chunks(own, rows, cols):
    pairs = [(rows * j + g, g * cols + j) for g in range(rows) for j in range(cols)]
    return lax.ppermute(own, ("grow", "gcol"), pairs)


def encode(first, partner, turn=0, mirrored=0, turned=0):
    return first + partner * 256 + (turn << 16) + (mirrored << 19) + (turned << 20) + (1 << 21)


def field(code, at, bits):
    return lax.bitwise_and(lax.shift_right_logical(code, at), (1 << bits) - 1)


def fill_table(widths, table, depth):
    at = jnp.int32(0)
    for p in range(widths.shape[0]):
        base = p * depth
        groups, rest = lax.shift_right_logical(widths[p], 3), lax.bitwise_and(widths[p], BLOCK - 1)
        few = jnp.where(rest < 5, 1, 0)

        def partner(c, at, base=base, groups=groups, few=few):
            level = lax.shift_right_logical(c, 3)
            for i in range(depth // BLOCK - 1):
                table[at + i] = encode(base + BLOCK * i, base + c, mirrored=1)
            at = at + level
            table[at] = encode(base + BLOCK * level, base + c)
            return at + jnp.where(level == groups, few, 0)

        at = lax.fori_loop(0, widths[p], partner, at)
        turned = groups + 1 - few
        for g in range(depth // BLOCK):
            for turn in range(5):
                table[at + turn] = encode(base + BLOCK * g, base + BLOCK * g, turn, int(0 < turn < 4), 1)
            at = at + jnp.where(g < turned, 5, 0)

    def clear(i, carry):
        table[at + i] = 0
        return carry

    lax.fori_loop(0, 2 * TILE, clear, 0, unroll=8)
    table[table.shape[0] - 1] = at


def partners(code, block, row):
    back = lax.bitwise_and(BLOCK - field(code, 16, 3), BLOCK - 1)
    return jnp.where(field(code, 20, 1) == 1, pltpu.roll(block, back, 0), row)


def stage_kernel(backs, opens, *refs):
    refs = list(refs)
    widths, core_ref = refs.pop(0), refs.pop(0)
    chunk_refs = [refs.pop(0) for _ in backs]
    core_v, panel, rho_a, rho_b, sems = refs[-5:]
    pairs, depth, chunk = chunk_refs[0].shape
    me = lax.axis_index("gcol")
    copies = []
    if opens:
        m_ref, table, own = refs[:3]
        copies.append(pltpu.make_async_copy(chunk_refs[0], own, sems.at[len(backs)]))
        copies[-1].start()
        chunk_refs = [own]
    else:
        table, m_ref = refs[0], refs[2 if len(refs) == 8 else 3]
    for u, back in enumerate(backs):
        rows = pl.ds(pl.multiple_of(lax.rem(me + 8 - back, 8) * chunk, chunk), chunk)
        copies.append(pltpu.make_async_copy(core_ref.at[rows], core_v.at[pl.ds(u * chunk, chunk)], sems.at[u]))
        copies[-1].start()
    if opens:
        fill_table(widths, table, depth)
        copies.pop(0).wait()
    for u in range(len(backs)):
        for p in range(pairs):
            panel[p * depth : (p + 1) * depth, u * chunk : (u + 1) * chunk] = chunk_refs[u][p].astype(F32)
    total = table[table.shape[0] - 1]

    def density(code):
        block = panel[pl.ds(pl.multiple_of(field(code, 0, 8), BLOCK), BLOCK), :]
        return block * partners(code, block, panel[pl.ds(field(code, 8, 8), 1), :])

    def build(rho, start):
        for i in range(TILE // 2):
            both = [density(table[start + 2 * i]), density(table[start + 2 * i + 1])]
            rho[16 * i : 16 * (i + 1), :] = jnp.concatenate(both, axis=0).astype(BF16)

    def multiply(rho, start, blocks):
        at = pl.ds(pl.multiple_of(start * BLOCK, 256), blocks * BLOCK)
        term = dot(rho[: blocks * BLOCK, :], core_v[...], NN)
        if opens:
            m_ref[at, :] = term
        else:
            m_ref[at, :] += term

    def step(rho, later, t):
        build(later, (t + 1) * TILE)
        multiply(rho, t * TILE, TILE)

    build(rho_a, 0)
    for copy in copies:
        copy.wait()
    tiles = (total + TILE // 2 - 1) // TILE

    def two_steps(i, carry):
        step(rho_a, rho_b, 2 * i)

        @pl.when(2 * i + 1 < tiles)
        def _():
            step(rho_b, rho_a, 2 * i + 1)

        return carry

    lax.fori_loop(0, (tiles + 1) // 2, two_steps, 0)
    odd = lax.rem(tiles, 2)
    for k, rho in enumerate((rho_a, rho_b)):

        @pl.when((total > tiles * TILE) & (odd == k))
        def _(rho=rho):
            multiply(rho, tiles * TILE, TILE // 2)


def end_kernel(widths, c0, c1, c2, c3, amps_ref, table, m_in, m_ref, out_ref, right, proj, terms, targets, acc):
    pairs, depth, chunk = c0.shape
    total = table[table.shape[0] - 1]
    for d, ref in enumerate((c0, c1, c2, c3)):
        at = pl.multiple_of(lax.rem(lax.axis_index("grow") + 4 - d, 4) * chunk, 128)
        for p in range(pairs):
            right[p * depth : (p + 1) * depth, pl.ds(at, chunk)] = ref[p]
    live = []
    for p in range(pairs):
        rows = slice(p * depth, (p + 1) * depth)
        spot = [lax.broadcasted_iota(jnp.int32, (depth, depth), k) < widths[p] for k in (0, 1)]
        live.append(spot[0] & spot[1])
        masked = jnp.where(live[p], amps_ref[p].astype(F32), 0.0).astype(BF16)
        proj[rows, :] = dot(masked, right[rows, :], NN).astype(BF16).astype(F32)
    acc[...] = jnp.zeros_like(acc)

    def finish(start, blocks):
        rows = blocks * BLOCK
        offset = lax.broadcasted_iota(jnp.int32, (BLOCK, 128), 0)

        def two(i, carry):
            plain, mirrored = [], []
            for k in range(2):
                code = table[start + 2 * i + k]
                first, partner = field(code, 0, 8), field(code, 8, 8)
                turn, turned = field(code, 16, 3), field(code, 20, 1)
                at = pl.multiple_of((start + 2 * i + k) * BLOCK, BLOCK)
                term = m_ref[pl.ds(at, BLOCK), :]
                block = proj[pl.ds(pl.multiple_of(first, BLOCK), BLOCK), :]
                plain.append(term * partners(code, block, proj[pl.ds(partner, 1), :]))
                mirrored.append(term * block)
                at = pl.multiple_of((2 * i + k) * BLOCK, BLOCK)
                targets[pl.ds(at, BLOCK), :] = offset + (first + 1024 * (field(code, 21, 1) - 1))
                over = turned * lax.bitwise_and(offset + turn, BLOCK - 1)
                targets[pl.ds(rows + at, BLOCK), :] = over + (partner + 1024 * (field(code, 19, 1) - 1))
            at = pl.multiple_of(16 * i, 16)
            terms[pl.ds(at, 16), :] = jnp.concatenate(plain, axis=0).astype(BF16)
            terms[pl.ds(rows + at, 16), :] = jnp.concatenate(mirrored, axis=0).astype(BF16)
            return carry

        lax.fori_loop(0, blocks // 2, two, 0, unroll=8)
        orbital = lax.broadcasted_iota(jnp.int32, (2 * rows, 128), 1)
        target = targets[: 2 * rows, :]
        pick = [jnp.where(target == orbital + 128 * k, 1.0, 0.0) for k in range(2)]
        pick = jnp.concatenate([pick[0], pick[1][:, : pairs * depth - 128]], axis=1).astype(BF16)
        acc[...] += dot(pick, dot(terms[: 2 * rows, :], right[...], NT).astype(BF16), TN)

    tiles = (total + TILE // 2 - 1) // TILE

    def full(t, carry):
        finish(t * TILE, TILE)
        return carry

    lax.fori_loop(0, tiles, full, 0)

    @pl.when(total > tiles * TILE)
    def _():
        finish(tiles * TILE, TILE // 2)

    for p in range(pairs):
        rows = slice(p * depth, (p + 1) * depth)
        out_ref[:, rows] = jnp.where(live[p], acc[rows, rows], 0.0)


VSPEC = pl.BlockSpec(memory_space=pltpu.VMEM)
SSPEC = pl.BlockSpec(memory_space=pltpu.SMEM)
HSPEC = pl.BlockSpec(memory_space=pltpu.HBM)


def settings(flops):
    return dict(
        cost_estimate=pl.CostEstimate(flops=flops, bytes_accessed=1 << 22, transcendentals=0),
        compiler_params=pltpu.CompilerParams(vmem_limit_bytes=LIMIT << 20),
    )


def stage(widths, core, chunks, backs, state, passed=None):
    pairs, depth, chunk = chunks[0].shape
    width = core.shape[1]
    opens = state is None
    inner = chunk * len(chunks)
    args = [widths, core, *chunks]
    specs = [SSPEC, HSPEC] + [HSPEC if opens else VSPEC] * len(chunks)
    if not opens:
        args += [state[1], state[0]]
        specs += [SSPEC, VSPEC]
    rows = pairs * depth
    groups = depth // BLOCK
    most = pairs * (BLOCK * groups * (groups - 1) // 2 + 5 * groups)
    most += -most % (TILE // 2)
    scratch = [
        pltpu.VMEM((inner, width), BF16),
        pltpu.VMEM((rows, inner), F32),
        pltpu.VMEM((TILE * BLOCK, inner), BF16),
        pltpu.VMEM((TILE * BLOCK, inner), BF16),
        pltpu.SemaphoreType.DMA((len(chunks) + 1,)),
    ]
    out, out_specs = [pltpu.VMEM((most * BLOCK, width), F32)], [VSPEC]
    aliases = {} if opens else {len(args) - 1: 0}
    if opens:
        scratch.insert(0, pltpu.VMEM((pairs, depth, chunk), BF16))
        out.append(jax.ShapeDtypeStruct((most + 3 * TILE,), jnp.int32))
        out_specs.append(SSPEC)
    if passed is not None:
        aliases[len(args)] = 1
        args.append(passed)
        specs.append(VSPEC)
        out.append(pltpu.VMEM(passed.shape, passed.dtype))
        out_specs.append(VSPEC)
    results = pl.pallas_call(
        functools.partial(stage_kernel, backs, opens),
        out_shape=out,
        in_specs=specs,
        out_specs=out_specs,
        scratch_shapes=scratch,
        input_output_aliases=aliases,
        **settings(2 * 2048 * inner * width),
    )(*args)
    return (results[0], results[1] if opens else state[1]), results[-1]


def ending(widths, columns, amplitudes, state):
    pairs, depth, chunk = columns[0].shape
    rows, width = pairs * depth, state[0].shape[1]
    return pl.pallas_call(
        end_kernel,
        out_shape=[pltpu.VMEM(state[0].shape, F32), jax.ShapeDtypeStruct((depth, rows), F32)],
        in_specs=[SSPEC] + [VSPEC] * (len(columns) + 1) + [SSPEC, VSPEC],
        out_specs=[VSPEC, VSPEC],
        scratch_shapes=[
            pltpu.VMEM((rows, width), BF16),
            pltpu.VMEM((rows, width), F32),
            pltpu.VMEM((2 * TILE * BLOCK, width), BF16),
            pltpu.VMEM((2 * TILE * BLOCK, 128), jnp.int32),
            pltpu.VMEM((rows, rows), F32),
        ],
        input_output_aliases={len(columns) + 3: 0},
        **settings(2 * 2048 * rows * width),
    )(widths, *columns, amplitudes, state[1], state[0])[1]


def local(core_matrix, pair_panels, amplitudes, pair_widths, batch_plan):
    rows, cols = lax.axis_size("grow"), lax.axis_size("gcol")
    core_matrix = pltpu.with_memory_space_constraint(core_matrix, pltpu.HBM)
    run = functools.partial(stage, pair_widths, core_matrix)
    right = lax.ppermute(pair_panels, "gcol", shift(cols, 1))
    left = lax.ppermute(pair_panels, "gcol", shift(cols, -1))
    column = column_chunks(pair_panels, rows, cols)
    state, _ = run([pltpu.with_memory_space_constraint(pair_panels, pltpu.HBM)], (0,), None)
    state, _ = run([right, left], (1, -1), state)
    right = lax.ppermute(right, "gcol", shift(cols, 1))
    left = lax.ppermute(left, "gcol", shift(cols, -1))
    state, column = run([right, left], (2, -2), state, column)
    right = lax.ppermute(right, "gcol", shift(cols, 1))
    left = lax.ppermute(left, "gcol", shift(cols, -1))
    last = lax.ppermute(right, "gcol", shift(cols, 1))
    state, _ = run([right, left, last], (3, -3, 4), state)
    columns = [column] + [lax.ppermute(column, "grow", shift(rows, d)) for d in range(1, rows)]
    parts = ending(pair_widths, columns, amplitudes, state)
    mine = lax.all_to_all(parts, ("grow", "gcol"), 0, 0, tiled=True).sum(axis=0)
    copies = jnp.broadcast_to(mine, (lax.axis_size("pair"), *mine.shape))
    every = lax.all_to_all(copies, "pair", 0, 0, tiled=True)
    every = every.reshape(-1, parts.shape[0])
    return every.at[batch_plan].get(mode="promise_in_bounds")


def solution(mesh):
    in_specs = (
        P("grow", "gcol"),
        P("pair", None, ("grow", "gcol")),
        P("pair", None, None),
        P("pair"),
        P("pair"),
    )
    out_specs = P("pair", ("grow", "gcol"))
    return jax.shard_map(local, mesh=mesh, in_specs=in_specs, out_specs=out_specs, check_vma=False)
```

```python
import functools

import jax
import jax.numpy as jnp
from jax import lax
from jax.experimental import pallas as pl
from jax.experimental.pallas import tpu as pltpu
from jax.sharding import PartitionSpec as P

F32 = jnp.float32
BF16 = jnp.bfloat16
NN = (((1,), (0,)), ((), ()))
NT = (((1,), (1,)), ((), ()))
TN = (((0,), (0,)), ((), ()))
BLOCK = 8
TILE = 64
LIMIT = 24


def dot(a, b, dims):
    return lax.dot_general(a, b, dims, preferred_element_type=F32)


def shift(size, by):
    return [(i, (i + by) % size) for i in range(size)]


def column_chunks(own, rows, cols):
    pairs = [(rows * j + g, g * cols + j) for g in range(rows) for j in range(cols)]
    return lax.ppermute(own, ("grow", "gcol"), pairs)


def encode(first, partner, turn=0, mirrored=0, turned=0):
    return first + partner * 256 + (turn << 16) + (mirrored << 19) + (turned << 20) + (1 << 21)


def field(code, at, bits):
    return lax.bitwise_and(lax.shift_right_logical(code, at), (1 << bits) - 1)


def fill_table(widths, table, depth):
    at = jnp.int32(0)
    for p in range(widths.shape[0]):
        base = p * depth
        groups, rest = lax.shift_right_logical(widths[p], 3), lax.bitwise_and(widths[p], BLOCK - 1)
        few = jnp.where(rest < 5, 1, 0)

        def partner(c, at, base=base, groups=groups, few=few):
            level = lax.shift_right_logical(c, 3)
            for i in range(depth // BLOCK - 1):
                table[at + i] = encode(base + BLOCK * i, base + c, mirrored=1)
            at = at + level
            table[at] = encode(base + BLOCK * level, base + c)
            return at + jnp.where(level == groups, few, 0)

        at = lax.fori_loop(0, widths[p], partner, at)
        turned = groups + 1 - few
        for g in range(depth // BLOCK):
            for turn in range(5):
                table[at + turn] = encode(base + BLOCK * g, base + BLOCK * g, turn, int(0 < turn < 4), 1)
            at = at + jnp.where(g < turned, 5, 0)

    def clear(i, carry):
        table[at + i] = 0
        return carry

    lax.fori_loop(0, 2 * TILE, clear, 0, unroll=8)
    table[table.shape[0] - 1] = at


def partners(code, block, row):
    back = lax.bitwise_and(BLOCK - field(code, 16, 3), BLOCK - 1)
    return jnp.where(field(code, 20, 1) == 1, pltpu.roll(block, back, 0), row)


def stage_kernel(backs, opens, *refs):
    refs = list(refs)
    widths, core_ref = refs.pop(0), refs.pop(0)
    chunk_refs = [refs.pop(0) for _ in backs]
    core_v, panel, rho_a, rho_b, sems = refs[-5:]
    pairs, depth, chunk = chunk_refs[0].shape
    me = lax.axis_index("gcol")
    copies = []
    if opens:
        m_ref, table, own = refs[:3]
        copies.append(pltpu.make_async_copy(chunk_refs[0], own, sems.at[len(backs)]))
        copies[-1].start()
        chunk_refs = [own]
    else:
        table, m_ref = refs[0], refs[2 if len(refs) == 8 else 3]
    for u, back in enumerate(backs):
        rows = pl.ds(pl.multiple_of(lax.rem(me + 8 - back, 8) * chunk, chunk), chunk)
        copies.append(pltpu.make_async_copy(core_ref.at[rows], core_v.at[pl.ds(u * chunk, chunk)], sems.at[u]))
        copies[-1].start()
    if opens:
        fill_table(widths, table, depth)
        copies.pop(0).wait()
    for u in range(len(backs)):
        for p in range(pairs):
            panel[p * depth : (p + 1) * depth, u * chunk : (u + 1) * chunk] = chunk_refs[u][p].astype(F32)
    total = table[table.shape[0] - 1]

    def density(code):
        block = panel[pl.ds(pl.multiple_of(field(code, 0, 8), BLOCK), BLOCK), :]
        return block * partners(code, block, panel[pl.ds(field(code, 8, 8), 1), :])

    def build(rho, start):
        for i in range(TILE // 2):
            both = [density(table[start + 2 * i]), density(table[start + 2 * i + 1])]
            rho[16 * i : 16 * (i + 1), :] = jnp.concatenate(both, axis=0).astype(BF16)

    def multiply(rho, start, blocks):
        at = pl.ds(pl.multiple_of(start * BLOCK, 256), blocks * BLOCK)
        term = dot(rho[: blocks * BLOCK, :], core_v[...], NN)
        if opens:
            m_ref[at, :] = term
        else:
            m_ref[at, :] += term

    def step(rho, later, t):
        build(later, (t + 1) * TILE)
        multiply(rho, t * TILE, TILE)

    build(rho_a, 0)
    for copy in copies:
        copy.wait()
    tiles = (total + TILE // 2 - 1) // TILE

    def two_steps(i, carry):
        step(rho_a, rho_b, 2 * i)

        @pl.when(2 * i + 1 < tiles)
        def _():
            step(rho_b, rho_a, 2 * i + 1)

        return carry

    lax.fori_loop(0, (tiles + 1) // 2, two_steps, 0)
    odd = lax.rem(tiles, 2)
    for k, rho in enumerate((rho_a, rho_b)):

        @pl.when((total > tiles * TILE) & (odd == k))
        def _(rho=rho):
            multiply(rho, tiles * TILE, TILE // 2)


def end_kernel(widths, c0, c1, c2, c3, amps_ref, m_in, m_ref, out_ref, right, proj, plain, mirror):
    pairs, depth, chunk = c0.shape
    for d, ref in enumerate((c0, c1, c2, c3)):
        at = pl.multiple_of(lax.rem(lax.axis_index("grow") + 4 - d, 4) * chunk, 128)
        for p in range(pairs):
            right[p * depth : (p + 1) * depth, pl.ds(at, chunk)] = ref[p]
    live = []
    for p in range(pairs):
        rows = slice(p * depth, (p + 1) * depth)
        spot = [lax.broadcasted_iota(jnp.int32, (depth, depth), k) < widths[p] for k in (0, 1)]
        live.append(spot[0] & spot[1])
        masked = jnp.where(live[p], amps_ref[p].astype(F32), 0.0).astype(BF16)
        proj[rows, :] = dot(masked, right[rows, :], NN).astype(BF16).astype(F32)
    plain[...] = jnp.zeros_like(plain)
    mirror[...] = jnp.zeros_like(mirror)
    half = plain.shape[1] // 2

    def group_rows(base, group):
        return pl.ds(pl.multiple_of(base + BLOCK * group, BLOCK), BLOCK)

    def term_rows(at):
        return pl.ds(pl.multiple_of(at * BLOCK, BLOCK), BLOCK)

    def spread(base, start, level, live_here, own, cols):
        blocks = level + own

        def partner(k, sums):
            c = base + BLOCK * level + k
            row = proj[pl.ds(c, 1), cols]
            sums, back = list(sums), None
            for i in range(blocks):
                term = m_ref[term_rows(start + k * blocks + i), cols]
                sums[i] = sums[i] + term * row
                if i < level:
                    image = term * proj[group_rows(base, i), cols]
                    back = image if back is None else back + image
            if level:
                mirror[pl.ds(c, 1), cols] = jnp.sum(back, axis=0, keepdims=True)
            return tuple(sums)

        unroll = 4 if isinstance(live_here, int) else 1
        sums = lax.fori_loop(0, live_here, partner, (jnp.zeros((BLOCK, half), F32),) * blocks, unroll=unroll)
        for i in range(blocks):
            plain[group_rows(base, i), cols] += sums[i]

    def turn_group(base, start, group, cols):
        block = proj[group_rows(base, group), cols]
        total = None
        for turn in range(5):
            term = m_ref[term_rows(start + turn), cols]
            ahead = pltpu.roll(block, BLOCK - turn, 0) if turn else block
            total = term * ahead if total is None else total + term * ahead
            if 0 < turn < 4:
                total = total + pltpu.roll(term * block, turn, 0)
        plain[group_rows(base, group), cols] += total

    def pair_sums(p, at):
        base = p * depth
        groups, rest = lax.shift_right_logical(widths[p], 3), lax.bitwise_and(widths[p], BLOCK - 1)
        few = jnp.where(rest < 5, 1, 0)
        for level in range(depth // BLOCK):
            here = jnp.clip(widths[p] - BLOCK * level, 0, BLOCK)
            extra = jnp.where(groups == level, few, 0)
            for own in range(2):
                if level + own:

                    @pl.when((extra == own) & (here > 0) & (here < BLOCK))
                    def _(at=at, level=level, here=here, own=own):
                        for h in range(2):
                            spread(base, at, level, here, own, slice(h * half, (h + 1) * half))

            if level:

                @pl.when(here == BLOCK)
                def _(at=at, level=level):
                    for h in range(2):
                        spread(base, at, level, BLOCK, 0, slice(h * half, (h + 1) * half))

            at = at + here * (level + extra)
        turned = groups + 1 - few

        def turns(g, carry):
            for h in range(2):
                turn_group(base, at + 5 * g, g, slice(h * half, (h + 1) * half))
            return carry

        lax.fori_loop(0, turned, turns, 0)
        return at + 5 * turned

    lax.fori_loop(0, pairs, pair_sums, jnp.int32(0))
    for p in range(pairs):
        rows = slice(p * depth, (p + 1) * depth)
        both = (plain[rows, :] + mirror[rows, :]).astype(BF16)
        out_ref[:, rows] = jnp.where(live[p], dot(both, right[rows, :], NT), 0.0)


VSPEC = pl.BlockSpec(memory_space=pltpu.VMEM)
SSPEC = pl.BlockSpec(memory_space=pltpu.SMEM)
HSPEC = pl.BlockSpec(memory_space=pltpu.HBM)


def settings(flops):
    return dict(
        cost_estimate=pl.CostEstimate(flops=flops, bytes_accessed=1 << 22, transcendentals=0),
        compiler_params=pltpu.CompilerParams(vmem_limit_bytes=LIMIT << 20),
    )


def stage(widths, core, chunks, backs, state, passed=None):
    pairs, depth, chunk = chunks[0].shape
    width = core.shape[1]
    opens = state is None
    inner = chunk * len(chunks)
    args = [widths, core, *chunks]
    specs = [SSPEC, HSPEC] + [HSPEC if opens else VSPEC] * len(chunks)
    if not opens:
        args += [state[1], state[0]]
        specs += [SSPEC, VSPEC]
    rows = pairs * depth
    groups = depth // BLOCK
    most = pairs * (BLOCK * groups * (groups - 1) // 2 + 5 * groups)
    most += -most % (TILE // 2)
    scratch = [
        pltpu.VMEM((inner, width), BF16),
        pltpu.VMEM((rows, inner), F32),
        pltpu.VMEM((TILE * BLOCK, inner), BF16),
        pltpu.VMEM((TILE * BLOCK, inner), BF16),
        pltpu.SemaphoreType.DMA((len(chunks) + 1,)),
    ]
    out, out_specs = [pltpu.VMEM((most * BLOCK, width), F32)], [VSPEC]
    aliases = {} if opens else {len(args) - 1: 0}
    if opens:
        scratch.insert(0, pltpu.VMEM((pairs, depth, chunk), BF16))
        out.append(jax.ShapeDtypeStruct((most + 3 * TILE,), jnp.int32))
        out_specs.append(SSPEC)
    if passed is not None:
        aliases[len(args)] = 1
        args.append(passed)
        specs.append(VSPEC)
        out.append(pltpu.VMEM(passed.shape, passed.dtype))
        out_specs.append(VSPEC)
    results = pl.pallas_call(
        functools.partial(stage_kernel, backs, opens),
        out_shape=out,
        in_specs=specs,
        out_specs=out_specs,
        scratch_shapes=scratch,
        input_output_aliases=aliases,
        **settings(2 * 2048 * inner * width),
    )(*args)
    return (results[0], results[1] if opens else state[1]), results[-1]


def ending(widths, columns, amplitudes, state):
    pairs, depth, chunk = columns[0].shape
    rows, width = pairs * depth, state[0].shape[1]
    return pl.pallas_call(
        end_kernel,
        out_shape=[pltpu.VMEM(state[0].shape, F32), jax.ShapeDtypeStruct((depth, rows), F32)],
        in_specs=[SSPEC] + [VSPEC] * (len(columns) + 2),
        out_specs=[VSPEC, VSPEC],
        scratch_shapes=[
            pltpu.VMEM((rows, width), BF16),
            pltpu.VMEM((rows, width), F32),
            pltpu.VMEM((rows, width), F32),
            pltpu.VMEM((rows, width), F32),
        ],
        input_output_aliases={len(columns) + 2: 0},
        **settings(2 * 2048 * rows * width),
    )(widths, *columns, amplitudes, state[0])[1]


def local(core_matrix, pair_panels, amplitudes, pair_widths, batch_plan):
    rows, cols = lax.axis_size("grow"), lax.axis_size("gcol")
    core_matrix = pltpu.with_memory_space_constraint(core_matrix, pltpu.HBM)
    run = functools.partial(stage, pair_widths, core_matrix)
    right = lax.ppermute(pair_panels, "gcol", shift(cols, 1))
    left = lax.ppermute(pair_panels, "gcol", shift(cols, -1))
    column = column_chunks(pair_panels, rows, cols)
    state, _ = run([pltpu.with_memory_space_constraint(pair_panels, pltpu.HBM)], (0,), None)
    state, _ = run([right, left], (1, -1), state)
    right = lax.ppermute(right, "gcol", shift(cols, 1))
    left = lax.ppermute(left, "gcol", shift(cols, -1))
    state, column = run([right, left], (2, -2), state, column)
    right = lax.ppermute(right, "gcol", shift(cols, 1))
    left = lax.ppermute(left, "gcol", shift(cols, -1))
    last = lax.ppermute(right, "gcol", shift(cols, 1))
    state, _ = run([right, left, last], (3, -3, 4), state)
    columns = [column] + [lax.ppermute(column, "grow", shift(rows, d)) for d in range(1, rows)]
    parts = ending(pair_widths, columns, amplitudes, state)
    mine = lax.all_to_all(parts, ("grow", "gcol"), 0, 0, tiled=True).sum(axis=0)
    copies = jnp.broadcast_to(mine, (lax.axis_size("pair"), *mine.shape))
    every = lax.all_to_all(copies, "pair", 0, 0, tiled=True)
    every = every.reshape(-1, parts.shape[0])
    return every.at[batch_plan].get(mode="promise_in_bounds")


def solution(mesh):
    in_specs = (
        P("grow", "gcol"),
        P("pair", None, ("grow", "gcol")),
        P("pair", None, None),
        P("pair"),
        P("pair"),
    )
    out_specs = P("pair", ("grow", "gcol"))
    return jax.shard_map(local, mesh=mesh, in_specs=in_specs, out_specs=out_specs, check_vma=False)
```
